32 devices in a mesh: dp: 16 (over z, y, x), mp: 2 (over core).
Axes of the slice: x: 2, y: 2, z: 4, core: 2. Of those that a mesh axis runs over, the one named last changes fastest.
Arguments:
- clean: float32 [64, 3, 4096], P(('dp', 'mp')), may hold values from -1 to 1
- noise: float32 [64, 3, 4096], P(('dp', 'mp')), may hold values from -12 to 12
- lowres: float32 [64, 3, 4096], P(('dp', 'mp')), may hold values from -1 to 1
- aug_noise: float32 [64, 3, 4096], P(('dp', 'mp')), may hold values from -5 to 5
- timesteps: int32 [64], P(('dp', 'mp')), may hold values from 0 to 999
- aug_levels: int32 [64], P(('dp', 'mp')), may hold values from 0 to 999
- lengths: int32 [64], P(('dp', 'mp')), may hold values from 1 to 128
- text: bfloat16 [64, 128, 4096], P(('dp', 'mp')), may hold values from -160 to 160
- w_stem: float32 [6, 128], replicated, may hold values from -2.5 to 2.5
- w_time: float32 [256, 256], replicated, may hold values from -0.375 to 0.375
- conv_one: bfloat16 [1152, 128], replicated, may hold values from -0.1875 to 0.1875
- conv_two: bfloat16 [1152, 128], replicated, may hold values from -0.1875 to 0.1875
- kv_weight: bfloat16 [4096, 256], P('mp'), may hold values from -0.09375 to 0.09375
- w_query: bfloat16 [128, 128], replicated, may hold values from -0.5 to 0.5
- w_output: bfloat16 [128, 128], replicated, may hold values from -0.5 to 0.5
- w_head: bfloat16 [3, 128], replicated, may hold values from -0.5 to 0.5
Outputs:
- conv_one_update: float32 [1152, 128], P(('dp', 'mp'))
- conv_two_update: float32 [1152, 128], P(('dp', 'mp'))
- kv_update: float32 [4096, 256], P('mp', 'dp')
- loss_mean: float32 [], replicated
The draws below stay inside these ranges and needn't reach their ends.
All inputs are finite; a program needn't handle non-finite values.
Results may differ from the reference program's by a relative error of at most 0.03.
The reference program's roundings to bfloat16 on the way count: a program that leaves them out, or rounds other values in their place, can miss the bound.
Values may be sent and summed in bfloat16 or wider, within the bound.
A program may use at most 128 MiB of HBM per device.

```python
import math
import jax
import jax.numpy as jnp
from jax import lax

S = 64
C = 128
GROUPS = 32
HEADS = 2
HEAD_DIM = 64
A = 128
L = 128
DT = 4096
FREQS = 64
STEPS = 1000
BATCH = 64


def draw_text(key, part):
    base = jax.random.normal(jax.random.fold_in(key, 11), (BATCH, L, DT), jnp.float32)
    base = jnp.clip(base, -4.0, 4.0)
    return base.astype(jnp.bfloat16)


def draw_noise(key, part):
    ramp = jnp.arange(BATCH, dtype=jnp.float32) / max(BATCH - 1, 1)
    spread = (1.0 + 2.0 * ramp)[:, None, None]
    base = jnp.clip(jax.random.normal(jax.random.fold_in(key, 22), (BATCH, 3, S * S), jnp.float32), -4.0, 4.0)
    return (base * spread).astype(jnp.float32)


def set_ends(entries, stream_key, least, high):
    longest = entries.shape.index(max(entries.shape))
    spots = []
    for shift in (0, 1):
        where = [jax.random.randint(jax.random.fold_in(stream_key, axis), (), 0, length) for axis, length in enumerate(entries.shape)]
        where[longest] = (where[longest] + shift) % entries.shape[longest]
        spots.append(tuple(where))
    return entries.at[spots[0]].set(least).at[spots[1]].set(high)


def steps_of(rng, extent, cuts, low, largest):
    def one(axis_at, shards_of):
        steps = jax.random.uniform(jax.random.fold_in(jax.random.fold_in(rng, 6), axis_at), (shards_of,), jnp.float32, low / len(cuts), largest / len(cuts))
        return jnp.repeat(jnp.exp(steps), extent[axis_at] // shards_of).reshape((-1,) + (1,) * (len(extent) - axis_at - 1))

    gain = one(*cuts[0])
    for cut in cuts[1:]:
        gain = gain * one(*cut)
    return gain


def gaussian(stream_key, extent, scale, limit, cuts=(), kind=jnp.bfloat16):
    values = scale * jax.random.normal(stream_key, extent, jnp.float32)
    if cuts:
        values = values * steps_of(stream_key, extent, cuts, -0.22, 0.18)
    return jnp.clip(values, -limit, limit).astype(kind)


def setup_inputs(seed: int = 0) -> dict:
    arg_keys = jax.random.split(jax.random.key(seed), 17)
    clean = jnp.clip(jax.random.uniform(arg_keys[0], (BATCH, 3, S * S), jnp.float32, -1.0, 1.0) * steps_of(arg_keys[0], (BATCH, 3, S * S), ((0, 32),), -0.4, 0.0), -1.0, 1.0)
    noise = draw_noise(jax.random.fold_in(arg_keys[16], 71), 0)
    lowres = jnp.clip(jax.random.uniform(arg_keys[2], (BATCH, 3, S * S), jnp.float32, -1.0, 1.0) * steps_of(arg_keys[2], (BATCH, 3, S * S), ((0, 32),), -0.4, 0.0), -1.0, 1.0)
    aug_noise = gaussian(arg_keys[3], (BATCH, 3, S * S), 1.0, 5.0, ((0, 32),), jnp.float32)
    timesteps = set_ends(jax.random.randint(arg_keys[4], (BATCH,), 0, STEPS), jax.random.fold_in(arg_keys[4], 1), 0, STEPS - 1).astype(jnp.int32)
    aug_levels = set_ends(jax.random.randint(arg_keys[5], (BATCH,), 0, STEPS), jax.random.fold_in(arg_keys[5], 1), 0, STEPS - 1).astype(jnp.int32)
    lengths = set_ends(jax.random.randint(arg_keys[6], (BATCH,), 1, L + 1), jax.random.fold_in(arg_keys[6], 1), 1, L).astype(jnp.int32)
    text = draw_text(jax.random.fold_in(arg_keys[16], 71), 0)
    w_stem = gaussian(arg_keys[8], (6, C), 6 ** -0.5, 2.5, (), jnp.float32)
    w_time = gaussian(arg_keys[9], (4 * FREQS, 2 * C), (4 * FREQS) ** -0.5, 0.375, (), jnp.float32)
    conv_one = gaussian(arg_keys[10], (9 * C, C), (9 * C) ** -0.5, 0.1875)
    conv_two = gaussian(arg_keys[11], (9 * C, C), (9 * C) ** -0.5, 0.1875)
    kv_weight = gaussian(arg_keys[12], (DT, 2 * A), DT ** -0.5, 0.09375, ((0, 2),))
    w_query = gaussian(arg_keys[13], (C, A), C ** -0.5, 0.5)
    w_output = gaussian(arg_keys[14], (A, C), A ** -0.5, 0.5)
    w_head = gaussian(arg_keys[15], (3, C), C ** -0.5, 0.5)
    return dict(clean=clean, noise=noise, lowres=lowres, aug_noise=aug_noise, timesteps=timesteps, aug_levels=aug_levels, lengths=lengths, text=text, w_stem=w_stem, w_time=w_time, conv_one=conv_one, conv_two=conv_two, kv_weight=kv_weight, w_query=w_query, w_output=w_output, w_head=w_head)


def signal_level(index):
    ratio = (index.astype(jnp.float32) / STEPS + 0.008) / 1.008
    cosine = jnp.cos(ratio * (math.pi / 2.0))
    return cosine * cosine

def sinusoid(index):
    freqs = jnp.exp(-math.log(10000.0) * jnp.arange(FREQS, dtype=jnp.float32) / FREQS)
    angles = index.astype(jnp.float32) * freqs
    return jnp.concatenate([jnp.sin(angles), jnp.cos(angles)])

def prepare(clean, noise, lowres, aug_noise, tstep, level, w_stem, w_time):
    signal = signal_level(tstep)
    aug_signal = signal_level(level)
    noisy = jnp.sqrt(signal) * clean + jnp.sqrt(1.0 - signal) * noise
    low_noisy = jnp.sqrt(aug_signal) * lowres + jnp.sqrt(1.0 - aug_signal) * aug_noise
    stacked = jnp.concatenate([noisy, low_noisy], axis=0)
    h_start = jnp.einsum('kp,kc->pc', stacked, w_stem, precision=lax.Precision.HIGHEST)
    feature = jnp.concatenate([sinusoid(tstep), sinusoid(level)])[None, :]
    embed = jax.nn.silu(jnp.dot(feature, w_time, precision=lax.Precision.HIGHEST))[0]
    channels = w_stem.shape[1]
    return (h_start, embed[:channels], embed[channels:])

def group_matrix(channels):
    members = channels // GROUPS
    labels = jnp.arange(channels) // members
    return (labels[:, None] == labels[None, :]).astype(jnp.float32) / members

def group_norm(values, grouping):
    average = jnp.dot(lax.optimization_barrier(jnp.mean(values, axis=0, keepdims=True)), grouping, precision=lax.Precision.HIGHEST)
    centred = values - average
    spread = jnp.dot(lax.optimization_barrier(jnp.mean(centred * centred, axis=0, keepdims=True)), grouping, precision=lax.Precision.HIGHEST)
    return centred * lax.rsqrt(spread + 1e-05)

def convolve(activation, weight):
    channels = weight.shape[1]
    kernel = weight.reshape(3, 3, channels, channels)
    picture = activation.reshape(1, S, S, channels)
    result = lax.conv_general_dilated(picture, kernel, (1, 1), 'SAME', dimension_numbers=('NHWC', 'HWIO', 'NHWC'), preferred_element_type=jnp.float32)
    return result.reshape(S * S, channels)

def image_loss(conv_one, conv_two, keys_values, h_start, scale, shift, keep, w_query, w_output, w_head, noise):
    channels = conv_one.shape[1]
    grouping = group_matrix(channels)
    act_one = jax.nn.silu(group_norm(h_start, grouping)).astype(jnp.bfloat16)
    conv_out_one = convolve(act_one, conv_one)
    act_two = jax.nn.silu(group_norm(conv_out_one, grouping) * (1.0 + scale) + shift).astype(jnp.bfloat16)
    h_mid = h_start + convolve(act_two, conv_two)
    normed = group_norm(h_mid, grouping).astype(jnp.bfloat16)
    queries = (jnp.dot(normed, w_query, preferred_element_type=jnp.float32) * HEAD_DIM ** (-0.5)).astype(jnp.bfloat16)
    width = w_query.shape[1]
    pieces = []
    for head_index in range(HEADS):
        lower = head_index * HEAD_DIM
        upper = lower + HEAD_DIM
        scores = jnp.dot(queries[:, lower:upper], keys_values[:, lower:upper].T, preferred_element_type=jnp.float32)
        scores = jnp.where(keep[None, :], scores, -1e+30)
        highest = lax.optimization_barrier(jnp.max(scores, axis=1, keepdims=True))
        weights = jnp.exp(scores - highest)
        probs = (weights / lax.optimization_barrier(jnp.sum(weights, axis=1, keepdims=True))).astype(jnp.bfloat16)
        pieces.append(jnp.dot(probs, keys_values[:, width + lower:width + upper], preferred_element_type=jnp.float32))
    attended = jnp.concatenate(pieces, axis=1).astype(jnp.bfloat16)
    h_out = h_mid + jnp.dot(attended, w_output, preferred_element_type=jnp.float32)
    pred = jnp.einsum('kc,pc->kp', w_head.astype(jnp.float32), h_out.astype(jnp.bfloat16).astype(jnp.float32))
    error = pred - noise
    return jnp.sum(error * error)

def normalize(grad):
    return grad * lax.rsqrt(jnp.mean(grad * grad) + 1e-06)

def reference(clean, noise, lowres, aug_noise, timesteps, aug_levels, lengths, text, w_stem, w_time, conv_one, conv_two, kv_weight, w_query, w_output, w_head):

    def visit(carry, items):
        grad_one, grad_two, grad_kv, total = carry
        clean_i, noise_i, low_i, aug_i, tstep, level, length, text_i = items
        h_start, scale, shift = prepare(clean_i, noise_i, low_i, aug_i, tstep, level, w_stem, w_time)
        keys_values = jnp.dot(text_i, kv_weight, preferred_element_type=jnp.float32).astype(jnp.bfloat16)
        keep = jnp.arange(text_i.shape[0]).astype(jnp.int32) < length
        value, pullback = jax.vjp(lambda first, second, third: image_loss(first, second, third, h_start, scale, shift, keep, w_query, w_output, w_head, noise_i), conv_one, conv_two, keys_values)
        part_one, part_two, part_kv = pullback(jnp.ones((), value.dtype))
        grad_kv = grad_kv + jnp.dot(text_i.T, part_kv, preferred_element_type=jnp.float32)
        return ((grad_one + part_one.astype(jnp.float32), grad_two + part_two.astype(jnp.float32), grad_kv, total + value), None)
    start = (jnp.zeros(conv_one.shape, jnp.float32), jnp.zeros(conv_two.shape, jnp.float32), jnp.zeros(kv_weight.shape, jnp.float32), jnp.zeros((), jnp.float32))
    finals, unused = lax.scan(visit, start, (clean, noise, lowres, aug_noise, timesteps, aug_levels, lengths, text))
    grad_one, grad_two, grad_kv, total = finals
    count = clean.shape[0] * clean.shape[1] * clean.shape[2]
    return (normalize(grad_one), normalize(grad_two), normalize(grad_kv), total / count)
```

```python
import functools
import math

import jax
import jax.numpy as jnp
from jax import lax
from jax.experimental import pallas as pl
from jax.experimental.pallas import tpu as pltpu
from jax.sharding import PartitionSpec as P

S = 64
GROUPS = 32
HEADS = 2
HEAD_DIM = 64
FREQS = 64
STEPS = 1000


def signal_level(index):
    ratio = (index.astype(jnp.float32) / STEPS + 0.008) / 1.008
    cosine = jnp.cos(ratio * (math.pi / 2.0))
    return cosine * cosine


def sinusoid(index):
    freqs = jnp.exp(-math.log(10000.0) * jnp.arange(FREQS, dtype=jnp.float32) / FREQS)
    angles = index.astype(jnp.float32) * freqs
    return jnp.concatenate([jnp.sin(angles), jnp.cos(angles)])


def prepare(clean, noise, lowres, aug_noise, tstep, level, w_stem, w_time):
    signal = signal_level(tstep)
    aug_signal = signal_level(level)
    noisy = jnp.sqrt(signal) * clean + jnp.sqrt(1.0 - signal) * noise
    low_noisy = jnp.sqrt(aug_signal) * lowres + jnp.sqrt(1.0 - aug_signal) * aug_noise
    stacked = jnp.concatenate([noisy, low_noisy], axis=0)
    h_start = jnp.einsum("kp,kc->pc", stacked, w_stem, precision=lax.Precision.HIGHEST)
    feature = jnp.concatenate([sinusoid(tstep), sinusoid(level)])[None, :]
    embed = jax.nn.silu(jnp.dot(feature, w_time, precision=lax.Precision.HIGHEST))[0]
    channels = w_stem.shape[1]
    return (h_start, embed[:channels], embed[channels:])


def group_matrix(channels):
    members = channels // GROUPS
    labels = jnp.arange(channels) // members
    return (labels[:, None] == labels[None, :]).astype(jnp.float32) / members


def group_norm(values, grouping):
    average = jnp.dot(
        jnp.mean(values, axis=0, keepdims=True), grouping, precision=lax.Precision.HIGHEST
    )
    centred = values - average
    spread = jnp.dot(
        jnp.mean(centred * centred, axis=0, keepdims=True),
        grouping,
        precision=lax.Precision.HIGHEST,
    )
    return centred * lax.rsqrt(spread + 1e-05)


def convolve(activation, weight):
    channels = weight.shape[1]
    kernel = weight.reshape(3, 3, channels, channels)
    picture = activation.reshape(1, S, S, channels)
    result = lax.conv_general_dilated(
        picture,
        kernel,
        (1, 1),
        "SAME",
        dimension_numbers=("NHWC", "HWIO", "NHWC"),
        preferred_element_type=jnp.float32,
    )
    return result.reshape(S * S, channels)


def image_loss(
    conv_one, conv_two, keys_values, h_start, scale, shift, keep, w_query, w_output, w_head, noise
):
    channels = conv_one.shape[1]
    grouping = group_matrix(channels)
    act_one = jax.nn.silu(group_norm(h_start, grouping)).astype(jnp.bfloat16)
    conv_out_one = convolve(act_one, conv_one)
    act_two = jax.nn.silu(group_norm(conv_out_one, grouping) * (1.0 + scale) + shift).astype(
        jnp.bfloat16
    )
    h_mid = h_start + convolve(act_two, conv_two)
    normed = group_norm(h_mid, grouping).astype(jnp.bfloat16)
    queries = (
        jnp.dot(normed, w_query, preferred_element_type=jnp.float32) * HEAD_DIM ** (-0.5)
    ).astype(jnp.bfloat16)
    width = w_query.shape[1]
    pieces = []
    for head_index in range(HEADS):
        lower = head_index * HEAD_DIM
        upper = lower + HEAD_DIM
        scores = jnp.dot(
            queries[:, lower:upper],
            keys_values[:, lower:upper].T,
            preferred_element_type=jnp.float32,
        )
        scores = jnp.where(keep[None, :], scores, -1e30)
        highest = jnp.max(scores, axis=1, keepdims=True)
        weights = jnp.exp(scores - highest)
        probs = (weights / jnp.sum(weights, axis=1, keepdims=True)).astype(jnp.bfloat16)
        pieces.append(
            jnp.dot(
                probs,
                keys_values[:, width + lower : width + upper],
                preferred_element_type=jnp.float32,
            )
        )
    attended = jnp.concatenate(pieces, axis=1).astype(jnp.bfloat16)
    h_out = h_mid + jnp.dot(attended, w_output, preferred_element_type=jnp.float32)
    pred = jnp.einsum(
        "kc,pc->kp", w_head, h_out.astype(jnp.bfloat16), preferred_element_type=jnp.float32
    )
    error = pred - noise
    return jnp.sum(error * error)


def exchange_kernel(
    n,
    mp_size,
    counts,
    conv_ref,
    kv_ref,
    loss_ref,
    conv_out,
    kv_out,
    stat_out,
    conv_in,
    kv_in,
    stat_in,
    stat_ref,
    conv_send,
    conv_recv,
    kv_send,
    kv_recv,
    stat_send,
    stat_recv,
):
    half = kv_out.shape[1]
    me = lax.axis_index("dp") * mp_size + lax.axis_index("mp")

    def target(k):
        return lax.rem(me + k + 1, n)

    def place(t):
        return (lax.div(t, mp_size), lax.rem(t, mp_size))

    def kv_block(t):
        column = pl.multiple_of(lax.rem(t, mp_size) * half, half)
        return kv_ref.at[lax.div(t, mp_size), :, pl.ds(column, half)]

    def remote(src, dst, send, recv, k, slot):
        return pltpu.make_async_remote_copy(
            src_ref=src,
            dst_ref=dst.at[slot],
            send_sem=send.at[k],
            recv_sem=recv.at[k],
            device_id=place(target(k)),
            device_id_type=pl.DeviceIdType.MESH,
        )

    def kv_copy(k):
        return remote(kv_block(target(k)), kv_in, kv_send, kv_recv, k, k)

    def conv_copy(k):
        return remote(conv_ref.at[target(k)], conv_in, conv_send, conv_recv, k, k)

    def stat_copy(k, slot):
        return remote(stat_ref, stat_in, stat_send, stat_recv, k, slot)

    def over_peers(step):
        def body(k, carry):
            step(k)
            return carry

        lax.fori_loop(0, n - 1, body, 0)

    barrier = pltpu.get_barrier_semaphore()
    over_peers(
        lambda k: pl.semaphore_signal(
            barrier,
            inc=1,
            device_id=place(target(k)),
            device_id_type=pl.DeviceIdType.MESH,
        )
    )
    pl.semaphore_wait(barrier, n - 1)

    def start(k):
        kv_copy(k).start()
        conv_copy(k).start()

    over_peers(start)
    own = pl.multiple_of(lax.rem(me, mp_size) * half, half)
    kv_out[...] = kv_ref[lax.div(me, mp_size), :, pl.ds(own, half)].astype(jnp.float32)
    conv_out[...] = conv_ref[me].astype(jnp.float32)

    def gather(k):
        kv_copy(k).wait_recv()
        kv_out[...] += kv_in[k].astype(jnp.float32)
        conv_copy(k).wait_recv()
        conv_out[...] += conv_in[k].astype(jnp.float32)

    over_peers(gather)

    def lanes(values):
        folded = jnp.sum(values * values, axis=0, keepdims=True)
        total = folded[:, :128]
        for piece in range(1, folded.shape[1] // 128):
            total = total + folded[:, piece * 128 : (piece + 1) * 128]
        return total

    stat_ref[...] = loss_ref[...]
    stat_ref[0:1, :] = lanes(conv_out[0])
    stat_ref[1:2, :] = lanes(conv_out[1])
    stat_ref[2:3, :] = lanes(kv_out[...])
    over_peers(lambda k: stat_copy(k, me).start())
    stat_in[me] = stat_ref[...]

    def add_stat(k):
        stat_copy(k, lax.rem(me + n - k - 1, n)).wait_recv()

    over_peers(add_stat)
    totals = jnp.sum(jnp.sum(stat_in[...], axis=0), axis=1, keepdims=True)
    stat_out[...] = jnp.broadcast_to(totals, stat_out.shape)
    conv_out[0] = conv_out[0] * lax.rsqrt(totals[0:1] / counts[0] + 1e-06)
    conv_out[1] = conv_out[1] * lax.rsqrt(totals[1:2] / counts[0] + 1e-06)
    kv_out[...] = kv_out[...] * lax.rsqrt(totals[2:3] / counts[1] + 1e-06)

    def finish(k):
        kv_copy(k).wait_send()
        conv_copy(k).wait_send()
        stat_copy(k, me).wait_send()

    over_peers(finish)


def exchange(conv_blocks, kv_blocks, loss, counts, mp_size):
    n = conv_blocks.shape[0]
    columns = kv_blocks.shape[1]
    half = kv_blocks.shape[2] // mp_size
    vmem = pl.BlockSpec(memory_space=pltpu.VMEM)
    return pl.pallas_call(
        functools.partial(exchange_kernel, n, mp_size, counts),
        out_shape=(
            jax.ShapeDtypeStruct(conv_blocks.shape[1:], jnp.float32),
            jax.ShapeDtypeStruct((columns, half), jnp.float32),
            jax.ShapeDtypeStruct(loss.shape, jnp.float32),
        ),
        in_specs=[vmem] * 3,
        out_specs=(vmem,) * 3,
        scratch_shapes=[
            pltpu.VMEM((n - 1,) + conv_blocks.shape[1:], conv_blocks.dtype),
            pltpu.VMEM((n - 1, columns, half), kv_blocks.dtype),
            pltpu.VMEM((n,) + loss.shape, jnp.float32),
            pltpu.VMEM(loss.shape, jnp.float32),
        ]
        + [pltpu.SemaphoreType.DMA((n - 1,))] * 6,
        compiler_params=pltpu.CompilerParams(collective_id=0, has_side_effects=True),
    )(conv_blocks, kv_blocks, loss)


def local(
    clean,
    noise,
    lowres,
    aug_noise,
    timesteps,
    aug_levels,
    lengths,
    text,
    w_stem,
    w_time,
    conv_one,
    conv_two,
    kv_weight,
    w_query,
    w_output,
    w_head,
):
    images = clean.shape[0]
    tokens = text.shape[1]
    features = text.shape[2]
    width = kv_weight.shape[1]
    half = kv_weight.shape[0]
    piece = lax.all_gather(kv_weight, "mp", axis=0, tiled=True)
    flat = jnp.dot(
        text.reshape(images * tokens, piece.shape[0]), piece, preferred_element_type=jnp.float32
    )
    summed = flat.reshape(images, tokens, width)
    keys_values = summed.astype(jnp.bfloat16)

    def one_image(items):
        clean_i, noise_i, low_i, aug_i, tstep, level, length, pairs = items
        h_start, scale, shift = prepare(
            clean_i, noise_i, low_i, aug_i, tstep, level, w_stem, w_time
        )
        keep = jnp.arange(tokens) < length
        value, pullback = jax.vjp(
            lambda first, second, third: image_loss(
                first,
                second,
                third,
                h_start,
                scale,
                shift,
                keep,
                w_query,
                w_output,
                w_head,
                noise_i,
            ),
            conv_one,
            conv_two,
            pairs,
        )
        part_one, part_two, part_kv = pullback(jnp.ones((), jnp.float32))
        return (part_one, part_two, part_kv, value)

    parts_one, parts_two, parts_kv, values = lax.map(
        one_image, (clean, noise, lowres, aug_noise, timesteps, aug_levels, lengths, keys_values)
    )
    local_one = jnp.sum(parts_one.astype(jnp.float32), axis=0)
    local_two = jnp.sum(parts_two.astype(jnp.float32), axis=0)
    dp_size = lax.axis_size("dp")
    mp_size = lax.axis_size("mp")
    devices = dp_size * mp_size
    turned = lax.dot_general(
        parts_kv.reshape(-1, width),
        text.reshape(-1, features),
        (((0,), (0,)), ((), ())),
        preferred_element_type=jnp.float32,
    ).astype(jnp.bfloat16)
    rows = conv_one.shape[0] // devices
    conv_blocks = jnp.stack(
        [
            local_one.reshape(devices, rows, conv_one.shape[1]),
            local_two.reshape(devices, rows, conv_one.shape[1]),
        ],
        axis=1,
    ).astype(jnp.bfloat16)
    loss = jnp.zeros((8, 128), jnp.float32).at[3, 0].set(jnp.sum(values))
    counts = (conv_one.shape[0] * conv_one.shape[1], half * mp_size * width)
    conv_updates, kv_turned, stats = exchange(
        conv_blocks,
        turned.reshape(dp_size, width // dp_size, features),
        loss,
        counts,
        mp_size,
    )
    loss_mean = stats[3, 0] / (images * devices * clean.shape[1] * clean.shape[2])
    return (conv_updates[0], conv_updates[1], kv_turned.T, loss_mean)


def solution(mesh):
    return jax.shard_map(
        local,
        mesh=mesh,
        in_specs=(
            P(("dp", "mp"), None, None),
            P(("dp", "mp"), None, None),
            P(("dp", "mp"), None, None),
            P(("dp", "mp"), None, None),
            P(("dp", "mp")),
            P(("dp", "mp")),
            P(("dp", "mp")),
            P(("dp", "mp"), None, None),
            P(),
            P(),
            P(),
            P(),
            P("mp", None),
            P(),
            P(),
            P(),
        ),
        out_specs=(P(("dp", "mp"), None), P(("dp", "mp"), None), P("mp", "dp"), P()),
        check_vma=False,
    )
```
